512 devices in a mesh: grp: 8 (over z), seq: 64 (over y, x, core).
Axes of the slice: x: 4, y: 8, z: 8, core: 2. Of those that a mesh axis runs over, the one named last changes fastest.
Arguments:
- queries: bfloat16 [8, 8192, 4608], P('grp', 'seq'), may hold values from -16 to 16
- latents: bfloat16 [8, 8192, 576], P('grp', 'seq'), may hold values from -6 to 6
- cotangent: bfloat16 [8, 8192, 4096], P('grp', 'seq'), may hold values from -6 to 6
- comp_weight: float32 [32, 576], replicated, may hold values from -1 to 1
- sel_idx: int32 [8, 128, 64], P('grp', 'seq'), may hold values from 0 to 255, as said below
- sel_count: int32 [8, 128], P('grp', 'seq'), may hold values from 0 to 64, as said below
Outputs:
- attended: bfloat16 [8, 8192, 4096], P('grp', 'seq')
- query_grads: bfloat16 [8, 8192, 4608], P('grp', 'seq')
- latent_grads: float32 [8, 8192, 576], P('grp', 'seq')
- comp_weight_grads: float32 [32, 576], replicated
The draws below stay inside these ranges and needn't reach their ends.
Inputs may be any that keep to these rules, and one draw needn't show every extreme that they name: `sel_idx`: in query block r the first sel_count entries are distinct compressed-latent numbers below r * 2; the other entries are 0 and unused. sel_count of query block r is at most min(64, r * 2); the last query block of every sequence reaches min(64, 254).
All inputs are finite; a program needn't handle non-finite values.
Results may differ from the reference program's by a relative error of at most 0.019.
Values may be sent and summed in bfloat16 or wider, within the bound.
No kernel may reach another device: no remote copies, remote signals or barrier semaphores. Data moves between devices by JAX's collectives and lax.ppermute only.
A program may use at most 64 MiB of HBM per device.

```python
import jax
import jax.numpy as jnp
from jax import lax

DL = 512
DR = 64
H = 8
QB = 64
CS = 32
SEL = 64
WIN = 512
DK = 576
GROUPS = 8
TOKENS = 8192
NCMP = 256
NQB = 128


def joint_fields(key):
    key_latent = jax.random.fold_in(key, 11)
    key_query = jax.random.fold_in(key, 12)
    latent_field = jnp.clip(jax.random.normal(key_latent, (GROUPS, TOKENS, DK), jnp.float32), -6.0, 6.0)
    query_field = jnp.clip(jax.random.normal(key_query, (GROUPS, TOKENS, H, DK), jnp.float32), -6.0, 6.0)
    return (latent_field, query_field)


def draw_queries(key, part):
    latent_field, query_field = joint_fields(key)
    return query_field.reshape(GROUPS, TOKENS, H * DK).astype(jnp.bfloat16)


def draw_latents(key, part):
    latent_field, query_field = joint_fields(key)
    return latent_field.astype(jnp.bfloat16)


def selection(key):
    key_order = jax.random.fold_in(key, 21)
    key_count = jax.random.fold_in(key, 22)
    block_ids = jnp.arange(NQB, dtype=jnp.int32)
    available = block_ids * (QB // CS)
    candidate = jnp.arange(NCMP, dtype=jnp.int32)
    random_ranks = jax.random.randint(key_order, (GROUPS, NQB, NCMP), 0, NCMP, dtype=jnp.int32)
    barred = jnp.where(candidate[None, :] >= available[:, None], NCMP * NCMP, 0).astype(jnp.int32)
    ranking = random_ranks * NCMP + candidate[None, None, :] + barred[None]
    ranked = jnp.argsort(ranking, axis=2, stable=True)[:, :, :SEL].astype(jnp.int32)
    wanted = jax.random.randint(key_count, (GROUPS, NQB), SEL // 2, SEL + 1, dtype=jnp.int32)
    wanted = jnp.where(block_ids[None, :] == NQB - 1, SEL, wanted)
    live_count = jnp.minimum(wanted, available[None, :]).astype(jnp.int32)
    slot_ids = jnp.arange(SEL, dtype=jnp.int32)
    chosen_ids = jnp.where(slot_ids[None, None, :] < live_count[:, :, None], ranked, 0).astype(jnp.int32)
    return (chosen_ids, live_count)


def draw_sel_idx(key, part):
    chosen_ids, live_count = selection(key)
    return chosen_ids


def draw_sel_count(key, part):
    chosen_ids, live_count = selection(key)
    return live_count


def steps_of(key, shape, cuts, smallest, largest):
    def one(dim, shards_of):
        draws = jax.random.uniform(jax.random.fold_in(jax.random.fold_in(key, 6), dim), (shards_of,), jnp.float32, smallest / len(cuts), largest / len(cuts))
        return jnp.repeat(jnp.exp(draws), shape[dim] // shards_of).reshape((-1,) + (1,) * (len(shape) - dim - 1))

    loudness = one(*cuts[0])
    for cut in cuts[1:]:
        loudness = loudness * one(*cut)
    return loudness


def scatter_about(own_key, shape, deviation, most, pieces=(), kind=jnp.bfloat16):
    array = jax.random.normal(own_key, shape, jnp.float32) * deviation
    if len(pieces) > 0:
        array = steps_of(own_key, shape, pieces, -0.22, 0.18) * array
    return jnp.clip(array, min=-most, max=most).astype(kind)


def setup_inputs(seed: int = 0) -> dict:
    key_of = jax.random.split(jax.random.key(seed), 7)
    return {
        "queries": draw_queries(jax.random.fold_in(key_of[6], 71), 0),
        "latents": draw_latents(jax.random.fold_in(key_of[6], 71), 0),
        "cotangent": scatter_about(key_of[2], (GROUPS, TOKENS, H * DL), 1.0, 6.0, ((0, 8), (1, 64))),
        "comp_weight": scatter_about(key_of[3], (CS, DK), CS ** -0.5, 1.0, (), jnp.float32),
        "sel_idx": draw_sel_idx(jax.random.fold_in(key_of[6], 71), 0),
        "sel_count": draw_sel_count(jax.random.fold_in(key_of[6], 71), 0),
    }


score_scale = 192.0 ** -0.5


def forward_block(query_rows, grad_rows, key_rows, allowed):
    scores = jnp.einsum("qhd,kd->qhk", query_rows.astype(jnp.float32), key_rows.astype(jnp.float32)) * score_scale
    scores = jnp.where(allowed[:, None, :], scores, -jnp.inf)
    row_max = jnp.max(scores, axis=2, keepdims=True)
    expo_part = jnp.exp(scores - row_max)
    row_sum = jnp.sum(expo_part, axis=2, keepdims=True)
    weights = expo_part / row_sum
    rounded = weights.astype(jnp.bfloat16)
    value_rows = key_rows[:, :DL]
    context = jnp.einsum("qhk,kd->qhd", rounded.astype(jnp.float32), value_rows.astype(jnp.float32))
    prob_grad = jnp.einsum("qhd,kd->qhk", grad_rows.astype(jnp.float32), value_rows.astype(jnp.float32))
    row_dot = jnp.sum(grad_rows.astype(jnp.float32) * context, axis=2, keepdims=True)
    dscore = (weights * (prob_grad - row_dot)).astype(jnp.bfloat16)
    query_grad = jnp.einsum("qhk,kd->qhd", dscore.astype(jnp.float32), key_rows.astype(jnp.float32)) * score_scale
    return context, query_grad, dscore, rounded


def key_terms(query_rows, grad_rows, dscore, rounded):
    key_grad = jnp.einsum("qhk,qhd->kd", dscore.astype(jnp.float32), query_rows.astype(jnp.float32)) * score_scale
    value_grad = jnp.einsum("qhk,qhd->kd", rounded.astype(jnp.float32), grad_rows.astype(jnp.float32))
    return key_grad + jnp.pad(value_grad, ((0, 0), (0, DR)))


def reference(queries, latents, cotangent, comp_weight, sel_idx, sel_count):
    slot_ids = jnp.arange(SEL, dtype=jnp.int32)
    offsets = jnp.arange(WIN + QB, dtype=jnp.int32)
    within = jnp.arange(QB, dtype=jnp.int32)

    def one_group(inputs):
        group_queries, group_latents, group_grad, group_idx, group_count = inputs
        query_all = group_queries.reshape(TOKENS, H, DK)
        grad_all = group_grad.reshape(TOKENS, H, DL)
        block_view = group_latents.astype(jnp.float32).reshape(NCMP, CS, DK)
        compressed = jnp.sum(block_view * comp_weight[None], axis=1).astype(jnp.bfloat16)
        padded = jnp.concatenate([jnp.zeros((WIN, DK), jnp.bfloat16), group_latents], axis=0)

        def block_step(state_pair, block_id):
            padded_grad, compressed_grad = state_pair
            first_row = (block_id * QB).astype(jnp.int32)
            query_rows = lax.dynamic_slice_in_dim(query_all, first_row, QB, 0)
            grad_rows = lax.dynamic_slice_in_dim(grad_all, first_row, QB, 0)
            window_rows = lax.dynamic_slice_in_dim(padded, first_row, WIN + QB, 0)
            chosen = group_idx[block_id]
            live_slots = slot_ids < group_count[block_id]
            picked = jnp.take(compressed, chosen, axis=0)
            query_pos = first_row + within
            key_pos = first_row - WIN + offsets
            window_ok = (key_pos[None, :] <= query_pos[:, None]) & (key_pos[None, :] > query_pos[:, None] - WIN) & (key_pos[None, :] >= 0)
            allowed = jnp.concatenate([jnp.broadcast_to(live_slots[None, :], (QB, SEL)), window_ok], axis=1)
            key_rows = jnp.concatenate([picked, window_rows], axis=0)
            context, query_grad, dscore, rounded = forward_block(query_rows, grad_rows, key_rows, allowed)
            key_grad = key_terms(query_rows, grad_rows, dscore, rounded)
            compressed_grad = compressed_grad.at[chosen].add(key_grad[:SEL] * live_slots[:, None].astype(jnp.float32))
            old_rows = lax.dynamic_slice_in_dim(padded_grad, first_row, WIN + QB, 0)
            padded_grad = lax.dynamic_update_slice_in_dim(padded_grad, old_rows + key_grad[SEL:], first_row, 0)
            return (padded_grad, compressed_grad), (context.astype(jnp.bfloat16), query_grad.astype(jnp.bfloat16))

        initial = (jnp.zeros((TOKENS + WIN, DK), jnp.float32), jnp.zeros((NCMP, DK), jnp.float32))
        (padded_grad, compressed_grad), (contexts, query_grads) = lax.scan(block_step, initial, jnp.arange(NQB, dtype=jnp.int32))
        latent_grad = padded_grad[WIN:] + (comp_weight[None] * compressed_grad[:, None, :]).reshape(TOKENS, DK)
        weight_grad = jnp.sum(compressed_grad[:, None, :] * block_view, axis=0)
        return contexts.reshape(TOKENS, H * DL), query_grads.reshape(TOKENS, H * DK), latent_grad, weight_grad

    attended, query_grads, latent_grads, weight_grads = lax.map(one_group, (queries, latents, cotangent, sel_idx, sel_count))
    return attended, query_grads, latent_grads, jnp.sum(weight_grads, axis=0)
```

```python
import jax
import jax.numpy as jnp
from jax import lax
from jax.sharding import Mesh, PartitionSpec as P

DL = 512
DR = 64
H = 8
QB = 64
CS = 32
SEL = 64
WIN = 512
DK = 576


score_scale = 192.0 ** (-0.5)


SEQ = ("y", "x", "c")
ROW = ("x", "c")


def shifted(block, axis, distance):
    devices = range(lax.axis_size(axis))
    route = [(i - distance, i) for i in devices if i - distance in devices]
    return lax.ppermute(block, axis, route)


def exchange(pieces, axis):
    return lax.all_to_all(pieces, axis, 0, 0, tiled=True)


def spread(piece, axis):
    return exchange(jnp.broadcast_to(piece[None], (lax.axis_size(axis),) + piece.shape), axis)


def sum_all(part):
    rows = part.shape[0] // lax.axis_size(ROW)
    pieces = part.astype(jnp.bfloat16).reshape(-1, rows, part.shape[1])
    total = jnp.sum(exchange(pieces, ROW).astype(jnp.float32), axis=0)
    for axis in ("y", "z"):
        total = jnp.sum(spread(total.astype(jnp.bfloat16), axis).astype(jnp.float32), axis=0)
    return spread(total.astype(jnp.bfloat16), ROW).reshape(part.shape).astype(jnp.float32)


def forward_block(query_rows, grad_rows, key_rows, allowed):
    scores = (
        jnp.einsum("qhd,kd->qhk", query_rows, key_rows, preferred_element_type=jnp.float32)
        * score_scale
    )
    scores = jnp.where(allowed[:, None, :], scores, -jnp.inf)
    row_max = jnp.max(scores, axis=2, keepdims=True)
    expo_part = jnp.exp(scores - row_max)
    row_sum = jnp.sum(expo_part, axis=2, keepdims=True)
    weights = expo_part / row_sum
    rounded = weights.astype(jnp.bfloat16)
    value_rows = key_rows[:, :DL]
    context = jnp.einsum("qhk,kd->qhd", rounded, value_rows, preferred_element_type=jnp.float32)
    prob_grad = jnp.einsum("qhd,kd->qhk", grad_rows, value_rows, preferred_element_type=jnp.float32)
    row_dot = jnp.sum(grad_rows.astype(jnp.float32) * context, axis=2, keepdims=True)
    dscore = (weights * (prob_grad - row_dot)).astype(jnp.bfloat16)
    query_grad = (
        jnp.einsum("qhk,kd->qhd", dscore, key_rows, preferred_element_type=jnp.float32)
        * score_scale
    )
    return (context, query_grad, dscore, rounded, row_max, row_sum, row_dot)


def key_terms(query_rows, grad_rows, dscore, rounded):
    key_grad = (
        jnp.einsum("qhk,qhd->kd", dscore, query_rows, preferred_element_type=jnp.float32)
        * score_scale
    )
    value_grad = jnp.einsum("qhk,qhd->kd", rounded, grad_rows, preferred_element_type=jnp.float32)
    return key_grad + jnp.pad(value_grad, ((0, 0), (0, DR)))


def body(queries, latents, cotangent, comp_weight, sel_idx, sel_count):
    tok_rows = latents.shape[1]
    base_pos = lax.axis_index(SEQ) * tok_rows
    local_blocks = tok_rows // QB
    comp_local = tok_rows // CS
    total_comp = comp_local * lax.axis_size(SEQ)
    hop_count = (WIN + tok_rows - 1) // tok_rows
    lead_rows = hop_count * tok_rows
    own_latent = latents[0]
    query_all = queries[0].reshape(tok_rows, H, DK)
    grad_all = cotangent[0].reshape(tok_rows, H, DL)
    block_view = own_latent.astype(jnp.float32).reshape(comp_local, CS, DK)
    compressed_local = jnp.sum(block_view * comp_weight[None], axis=1).astype(jnp.bfloat16)
    compressed = spread(compressed_local, SEQ).reshape(total_comp, DK)
    earlier = []
    for distance in range(hop_count, 0, -1):
        earlier.append(shifted(own_latent, SEQ, distance))
    extended = jnp.concatenate(earlier + [own_latent], axis=0)
    ext_grad = jnp.zeros((lead_rows + tok_rows, DK), jnp.float32)
    comp_ids = jnp.arange(total_comp, dtype=jnp.int32)
    slot_ids = jnp.arange(SEL, dtype=jnp.int32)
    within = jnp.arange(QB, dtype=jnp.int32)
    offsets = jnp.arange(WIN + QB, dtype=jnp.int32)
    comp_grad_full = jnp.zeros((total_comp, DK), jnp.float32)
    contexts = []
    query_grads = []
    for block_id in range(local_blocks):
        first_row = block_id * QB
        query_rows = query_all[first_row : first_row + QB]
        grad_rows = grad_all[first_row : first_row + QB]
        window_start = first_row + lead_rows - WIN
        window_rows = extended[window_start : window_start + WIN + QB]
        query_pos = base_pos + first_row + within
        key_pos = base_pos + first_row - WIN + offsets
        window_ok = (
            (key_pos[None, :] <= query_pos[:, None])
            & (key_pos[None, :] > query_pos[:, None] - WIN)
            & (key_pos[None, :] >= 0)
        )
        chosen = sel_idx[0, block_id]
        live_slots = slot_ids < sel_count[0, block_id]
        one_hot = (chosen[:, None] == comp_ids[None, :]) & live_slots[:, None]
        picked = jnp.take(compressed, chosen, axis=0)
        key_rows = jnp.concatenate([picked, window_rows], axis=0)
        allowed = jnp.concatenate(
            [jnp.broadcast_to(live_slots[None, :], (QB, SEL)), window_ok], axis=1
        )
        context, query_grad, dscore, rounded, row_max, row_sum, row_dot = forward_block(
            query_rows, grad_rows, key_rows, allowed
        )
        key_grad = key_terms(query_rows, grad_rows, dscore, rounded)
        comp_grad_full = comp_grad_full + jnp.einsum(
            "sc,sd->cd",
            one_hot.astype(jnp.float32),
            key_grad[:SEL],
            precision=lax.Precision.HIGHEST,
        )
        window_grad = key_grad[SEL:]
        ext_grad = ext_grad.at[window_start : window_start + WIN + QB].add(window_grad)
        contexts.append(context.astype(jnp.bfloat16).reshape(QB, H * DL))
        query_grads.append(query_grad.astype(jnp.bfloat16).reshape(QB, H * DK))
    comp_pieces = comp_grad_full.astype(jnp.bfloat16).reshape(-1, comp_local, DK)
    comp_grad = jnp.sum(exchange(comp_pieces, SEQ).astype(jnp.float32), axis=0)
    latent_grad = ext_grad[lead_rows:]
    for distance in range(hop_count, 0, -1):
        segment_start = (hop_count - distance) * tok_rows
        segment = ext_grad[segment_start : segment_start + tok_rows]
        latent_grad = latent_grad + shifted(segment.astype(jnp.bfloat16), SEQ, -distance).astype(
            segment.dtype
        )
    latent_grad = latent_grad + (comp_weight[None] * comp_grad[:, None, :]).reshape(tok_rows, DK)
    weight_part = jnp.sum(comp_grad[:, None, :] * block_view, axis=0)
    weight_grad = sum_all(weight_part)
    attended = jnp.concatenate(contexts, axis=0)[None]
    query_out = jnp.concatenate(query_grads, axis=0)[None]
    return (attended, query_out, latent_grad[None], weight_grad)


def solution(mesh):
    torus = Mesh(mesh.devices.reshape(mesh.shape["grp"], -1, 4, 2), ("z", "y", "x", "c"))
    split = P("z", SEQ, None)
    in_specs = (split, split, split, P(), split, P("z", SEQ))
    out_specs = (split, split, split, P())
    return jax.shard_map(body, mesh=torus, in_specs=in_specs, out_specs=out_specs, check_vma=False)
```

```python
import jax
import jax.numpy as jnp
from jax import lax
from jax.experimental import pallas as pl
from jax.experimental.pallas import tpu as pltpu
from jax.sharding import Mesh, PartitionSpec as P

DL = 512
DR = 64
H = 8
QB = 64
CS = 32
SEL = 64
WIN = 512
DK = 576

ROWS = 128
BACK = WIN // ROWS
OWN = ROWS // CS
PEERS = 64
HALF = DK // 2
WKEYS = WIN + ROWS
KEYS = WKEYS + 2 * SEL
PAD = DR

SEQ = ("y", "x", "c")
ROW = ("x", "c")

score_scale = 192.0 ** (-0.5)
F32 = jnp.float32
BF16 = jnp.bfloat16
VMEM = pl.BlockSpec(memory_space=pltpu.VMEM)
SMEM = pl.BlockSpec(memory_space=pltpu.SMEM)


def iota(shape, dim):
    return lax.broadcasted_iota(jnp.int32, shape, dim)


def dot_nn(a, b, **kw):
    return lax.dot_general(a, b, (((1,), (0,)), ((), ())), preferred_element_type=F32, **kw)


def dot_nt(a, b, **kw):
    return lax.dot_general(a, b, (((1,), (1,)), ((), ())), preferred_element_type=F32, **kw)


def dot_tn(a, b, **kw):
    return lax.dot_general(a, b, (((0,), (0,)), ((), ())), preferred_element_type=F32, **kw)


EXACT = dict(precision=lax.Precision.HIGHEST)


def spread_weight(weight):
    return dot_tn(weight, (iota((CS, ROWS), 1) % CS == iota((CS, ROWS), 0)).astype(F32), **EXACT)


def piece_of(half):
    return (iota((2 * OWN, ROWS), 1) // CS == iota((2 * OWN, ROWS), 0) - OWN * half).astype(F32)


def compress_kernel(own_ref, weight_ref, out_ref):
    terms = own_ref[...].astype(F32) * spread_weight(weight_ref[...])
    piece = dot_nt(piece_of(0), terms[:HALF], **EXACT) + dot_nt(piece_of(1), terms[HALF:], **EXACT)
    out_ref[...] = jnp.broadcast_to(piece.astype(BF16)[None], out_ref.shape)


def picked_rows(chosen, half):
    row = iota((2 * OWN * PEERS, 2 * SEL), 0)
    block = OWN * (row // (2 * OWN)) + row % (2 * OWN) - OWN * half
    inside = (row % (2 * OWN)) // OWN == half
    return ((block == chosen) & inside).astype(F32).astype(BF16)


def attend_kernel(
    place_ref, chosen_ref, w4_ref, w3_ref, w2_ref, w1_ref, own_ref, comp_ref, query_ref, grad_ref,
    attended_ref, query_out_ref, comp_out_ref, g4_ref, g3_ref, g2_ref, g1_ref, g0_ref,
    key_ref, query_t_ref, grad_t_ref, dscore_ref, prob_ref,
):
    place = place_ref[0]
    chosen = chosen_ref[...]
    key_ref[:PAD, :] = jnp.zeros((PAD, KEYS), BF16)
    key_ref[PAD + DK :, :] = jnp.zeros((PAD, KEYS), BF16)
    for i, ref in enumerate((w4_ref, w3_ref, w2_ref, w1_ref, own_ref)):
        key_ref[PAD : PAD + DK, i * ROWS : (i + 1) * ROWS] = ref[...]
    pieces = comp_ref[...].reshape(2 * OWN * PEERS, HALF)
    first, second = picked_rows(chosen, 0), picked_rows(chosen, 1)
    key_ref[PAD : PAD + HALF, WKEYS:] = dot_tn(pieces, first).astype(BF16)
    key_ref[PAD + HALF : PAD + DK, WKEYS:] = dot_tn(pieces, second).astype(BF16)

    token = iota((ROWS, KEYS), 0)
    key = iota((ROWS, KEYS), 1)
    near = (key <= token + WIN) & (key > token) & (key >= WIN - place * ROWS)
    picked = (key - WKEYS) // SEL == token // QB
    live = jnp.broadcast_to(chosen >= 0, (ROWS, 2 * SEL))
    live = jnp.concatenate([jnp.zeros((ROWS, WKEYS), jnp.int32), live.astype(jnp.int32)], axis=1) > 0
    allowed = jnp.where(key < WKEYS, near.astype(jnp.int32), (picked & live).astype(jnp.int32)) > 0
    values = key_ref[PAD : PAD + DL, :]

    for pair in range(H // 2):
        left = pair * 2 * DK
        query_pair = query_ref[:, left : left + 2 * DK]
        query_pair_t = query_pair.T
        for odd in range(2):
            head = 2 * pair + odd
            lane = head * ROWS
            query_t_ref[:, lane : lane + ROWS] = query_pair_t[odd * DK : (odd + 1) * DK]
            grad_rows = grad_ref[:, head * DL : (head + 1) * DL]
            grad_t_ref[:, lane : lane + ROWS] = grad_rows.T
            keys = key_ref[:DK + PAD, :] if odd else key_ref[PAD:, :]
            query_rows = query_pair[:, DL:] if odd else query_pair[:, : DK + PAD]
            scores = jnp.where(allowed, dot_nn(query_rows, keys) * score_scale, -1e30)
            expo = jnp.exp(scores - jnp.max(scores, axis=1, keepdims=True))
            weights = expo * (1.0 / jnp.sum(expo, axis=1, keepdims=True))
            rounded = weights.astype(BF16)
            context = dot_nt(rounded, values)
            prob_grad = dot_nn(grad_rows, values)
            row_dot = jnp.sum(grad_rows.astype(F32) * context, axis=1, keepdims=True)
            dscore = (weights * (prob_grad - row_dot)).astype(BF16)
            query_grad = dot_nt(dscore, keys) * score_scale
            attended_ref[:, head * DL : (head + 1) * DL] = context.astype(BF16)
            dscore_ref[lane : lane + ROWS, :] = dscore
            prob_ref[lane : lane + ROWS, :] = rounded
            if odd:
                middle = before[:, DL:] + query_grad[:, : DK + PAD - DL]
                query_out_ref[:, left : left + DL] = before[:, :DL].astype(BF16)
                query_out_ref[:, left + DL : left + DK + PAD] = middle.astype(BF16)
                query_out_ref[:, left + DK + PAD : left + 2 * DK] = query_grad[:, DK + PAD - DL :].astype(BF16)
            before = query_grad

    dscore, rounded = dscore_ref[...], prob_ref[...]
    key_grad = dot_nn(query_t_ref[...], dscore) * score_scale
    value_grad = dot_nn(grad_t_ref[...], rounded)
    total = jnp.concatenate([key_grad[:DL] + value_grad, key_grad[DL:]], axis=0)
    for i, ref in enumerate((g4_ref, g3_ref, g2_ref, g1_ref, g0_ref)):
        ref[...] = total[:, i * ROWS : (i + 1) * ROWS].astype(ref.dtype)
    picked_grad = total[:, WKEYS:].astype(BF16)
    comp = dot_nt(first, picked_grad[:HALF]) + dot_nt(second, picked_grad[HALF:])
    comp_out_ref[...] = comp.astype(BF16).reshape(comp_out_ref.shape)


def weight_kernel(comp_ref, own_ref, comp_out_ref, weight_out_ref):
    comp = jnp.sum(comp_ref[...].astype(F32), axis=0)
    comp_out_ref[...] = comp
    own = own_ref[...].astype(F32)
    fold = (iota((CS, ROWS), 1) % CS == iota((CS, ROWS), 0)).astype(F32)
    halves = []
    for half in range(2):
        wide = dot_tn(comp, piece_of(half), **EXACT)
        halves.append(dot_nt(fold, wide * own[half * HALF : (half + 1) * HALF], **EXACT))
    part = jnp.concatenate(halves, axis=1).astype(BF16)
    for i in range(weight_out_ref.shape[0]):
        weight_out_ref[i] = part[OWN * i : OWN * (i + 1)]


def latent_kernel(comp_ref, weight_ref, g0_ref, r1_ref, r2_ref, r3_ref, r4_ref, out_ref):
    comp = comp_ref[...]
    wide = jnp.concatenate([dot_tn(comp, piece_of(half), **EXACT) for half in range(2)], axis=0)
    total = g0_ref[...] + wide * spread_weight(weight_ref[...])
    for ref in (r1_ref, r2_ref, r3_ref, r4_ref):
        total = total + ref[...].astype(F32)
    out_ref[...] = total


def sum_kernel(part_ref, out_ref):
    total = jnp.sum(part_ref[...].astype(F32), axis=0, keepdims=True)
    out_ref[...] = jnp.broadcast_to(total, out_ref.shape).astype(out_ref.dtype)


def call(kernel, outs, in_specs, *args, scratch=(), flops=0):
    shapes = [jax.ShapeDtypeStruct(shape, dtype) for shape, dtype in outs]
    nbytes = sum(a.size * a.dtype.itemsize for a in args) + sum(s.size * s.dtype.itemsize for s in shapes)
    return pl.pallas_call(
        kernel,
        out_shape=shapes,
        in_specs=in_specs,
        out_specs=[VMEM] * len(shapes),
        scratch_shapes=scratch,
        cost_estimate=pl.CostEstimate(flops=flops, bytes_accessed=nbytes, transcendentals=0),
    )(*args)


def attend(place, chosen, windows, own, gathered, query_rows, grad_rows):
    seg = (DK, ROWS)
    rows = H * ROWS
    return call(
        attend_kernel,
        [((ROWS, H * DL), BF16), ((ROWS, H * DK), BF16), ((PEERS, 2 * OWN, HALF), BF16)]
        + [(seg, BF16)] * BACK + [(seg, F32)],
        [SMEM] + [VMEM] * 9,
        place, chosen, *windows, own, gathered, query_rows, grad_rows,
        scratch=[
            pltpu.VMEM((DK + 2 * PAD, KEYS), BF16),
            pltpu.VMEM((DK, rows), BF16),
            pltpu.VMEM((DL, rows), BF16),
            pltpu.VMEM((rows, KEYS), BF16),
            pltpu.VMEM((rows, KEYS), BF16),
        ],
        flops=2 * rows * KEYS * 6 * DK,
    )


def shifted(block, distance):
    devices = range(PEERS)
    route = [(i - distance, i) for i in devices if i - distance in devices]
    return lax.ppermute(block, SEQ, route)


def exchange(pieces, axis):
    return lax.all_to_all(pieces, axis, 0, 0, tiled=True)


def body(queries, latents, cotangent, comp_weight, sel_idx, sel_count):
    own = latents[0].T
    place = lax.axis_index(SEQ).astype(jnp.int32).reshape(1)
    slots = jnp.arange(SEL, dtype=jnp.int32)
    chosen = jnp.where(slots[None, :] < sel_count[0][:, None], sel_idx[0], -1).reshape(1, 2 * SEL)
    piece_shape = ((PEERS, 2 * OWN, HALF), BF16)
    (pieces,) = call(compress_kernel, [piece_shape], [VMEM] * 2, own, comp_weight)
    gathered = exchange(pieces, SEQ)
    windows = [shifted(own, distance) for distance in range(BACK, 0, -1)]
    attended, query_out, comp_pieces, *sends, g0 = attend(
        place, chosen, windows, own, gathered, queries[0], cotangent[0]
    )
    comp_parts = exchange(comp_pieces, SEQ)
    received = [shifted(sends[BACK - distance], -distance) for distance in range(1, BACK + 1)]
    comp, part = call(
        weight_kernel,
        [((2 * OWN, HALF), F32), ((8, OWN, DK), BF16)],
        [VMEM] * 2,
        comp_parts, own,
    )
    for axis in (ROW, "y", "z"):
        (part,) = call(sum_kernel, [((8, OWN, DK), BF16)], [VMEM], exchange(part, axis))
    weight_grad = exchange(part, ROW).reshape(CS, DK).astype(F32)
    (latent_grad,) = call(latent_kernel, [((DK, ROWS), F32)], [VMEM] * 7, comp, comp_weight, g0, *received)
    return (attended[None], query_out[None], latent_grad.T[None], weight_grad)


def solution(mesh):
    torus = Mesh(mesh.devices.reshape(mesh.shape["grp"], -1, 4, 2), ("z", "y", "x", "c"))
    split = P("z", SEQ, None)
    in_specs = (split, split, split, P(), split, P("z", SEQ))
    out_specs = (split, split, split, P())
    return jax.shard_map(body, mesh=torus, in_specs=in_specs, out_specs=out_specs, check_vma=False)
```

```python
import jax
import jax.numpy as jnp
from jax import lax
from jax.experimental import pallas as pl
from jax.experimental.pallas import tpu as pltpu
from jax.sharding import Mesh, PartitionSpec as P

DL = 512
DR = 64
H = 8
QB = 64
CS = 32
SEL = 64
WIN = 512
DK = 576

ROWS = 128
BACK = WIN // ROWS
OWN = ROWS // CS
PEERS = 64
WKEYS = WIN + ROWS
KEYS = WKEYS + 2 * SEL
PAD = DR

SEQ = ("y", "x", "c")
ROW = ("x", "c")

score_scale = 192.0 ** (-0.5)
F32 = jnp.float32
BF16 = jnp.bfloat16
VMEM = pl.BlockSpec(memory_space=pltpu.VMEM)
ANY = pl.BlockSpec(memory_space=pl.ANY)
SMEM = pl.BlockSpec(memory_space=pltpu.SMEM)


def iota(shape, dim):
    return lax.broadcasted_iota(jnp.int32, shape, dim)


def dot_nn(a, b, **kw):
    return lax.dot_general(a, b, (((1,), (0,)), ((), ())), preferred_element_type=F32, **kw)


def dot_nt(a, b, **kw):
    return lax.dot_general(a, b, (((1,), (1,)), ((), ())), preferred_element_type=F32, **kw)


def dot_tn(a, b, **kw):
    return lax.dot_general(a, b, (((0,), (0,)), ((), ())), preferred_element_type=F32, **kw)


EXACT = dict(precision=lax.Precision.HIGHEST)


def spread_weight(weight):
    return dot_tn(weight, (iota((CS, ROWS), 1) % CS == iota((CS, ROWS), 0)).astype(F32), **EXACT)


def owner():
    return (iota((OWN, ROWS), 1) // CS == iota((OWN, ROWS), 0)).astype(F32)


def compress_kernel(own_ref, weight_ref, out_ref):
    terms = own_ref[...].astype(F32) * spread_weight(weight_ref[...])
    piece = dot_nt(owner(), terms, **EXACT)
    out_ref[...] = jnp.broadcast_to(piece.astype(BF16)[None], out_ref.shape)


def pack_kernel(place_ref, own_ref, w2_ref, w4_ref, out_ref):
    first = place_ref[0] % 2 == 0
    w2 = w2_ref[...]
    out_ref[0] = jnp.where(first, w2, w4_ref[...])
    out_ref[1] = jnp.where(first, own_ref[...], w2)


def merge_kernel(place_ref, swap_ref, g2_ref, g4_ref, out2_ref, out4_ref):
    first = place_ref[0] % 2 == 0
    near, far = swap_ref[0].astype(F32), swap_ref[1].astype(F32)
    out2_ref[...] = (g2_ref[...] + jnp.where(first, far, near)).astype(BF16)
    out4_ref[...] = (g4_ref[...] + jnp.where(first, 0.0, far)).astype(BF16)


def attend_kernel(
    place_ref, chosen_ref, w4_ref, w2_ref, swap_ref, own_ref, comp_ref, query_ref, grad_ref,
    attended_ref, query_out_ref, comp_out_ref, swap_out_ref, g4_ref, g2_ref, g0_ref,
    key_ref, query_t_ref, grad_t_ref, dscore_ref, prob_ref,
):
    place = place_ref[0]
    chosen = chosen_ref[...]
    key_ref[:PAD, :] = jnp.zeros((PAD, KEYS), BF16)
    key_ref[PAD + DK :, :] = jnp.zeros((PAD, KEYS), BF16)
    for i, ref in enumerate((w4_ref, swap_ref.at[0], w2_ref, swap_ref.at[1], own_ref)):
        key_ref[PAD : PAD + DK, i * ROWS : (i + 1) * ROWS] = ref[...]
    picks = (iota((OWN * PEERS, 2 * SEL), 0) == chosen).astype(F32).astype(BF16)
    pieces = comp_ref[...].reshape(OWN * PEERS, DK)
    key_ref[PAD : PAD + DK, WKEYS:] = dot_tn(pieces, picks).astype(BF16)

    token = iota((ROWS, KEYS), 0)
    key = iota((ROWS, KEYS), 1)
    near = (key <= token + WIN) & (key > token) & (key >= WIN - place * ROWS)
    picked = (key - WKEYS) // SEL == token // QB
    live = jnp.broadcast_to(chosen >= 0, (ROWS, 2 * SEL))
    live = jnp.concatenate([jnp.zeros((ROWS, WKEYS), jnp.int32), live.astype(jnp.int32)], axis=1) > 0
    allowed = jnp.where(key < WKEYS, near.astype(jnp.int32), (picked & live).astype(jnp.int32)) > 0
    values = key_ref[PAD : PAD + DL, :]

    for pair in range(H // 2):
        left = pair * 2 * DK
        query_pair = query_ref[:, left : left + 2 * DK]
        query_pair_t = query_pair.T
        for odd in range(2):
            head = 2 * pair + odd
            lane = head * ROWS
            query_t_ref[:, lane : lane + ROWS] = query_pair_t[odd * DK : (odd + 1) * DK]
            grad_rows = grad_ref[:, head * DL : (head + 1) * DL]
            grad_t_ref[:, lane : lane + ROWS] = grad_rows.T
            keys = key_ref[:DK + PAD, :] if odd else key_ref[PAD:, :]
            query_rows = query_pair[:, DL:] if odd else query_pair[:, : DK + PAD]
            scores = jnp.where(allowed, dot_nn(query_rows, keys) * score_scale, -1e30)
            expo = jnp.exp(scores - jnp.max(scores, axis=1, keepdims=True))
            weights = expo * (1.0 / jnp.sum(expo, axis=1, keepdims=True))
            rounded = weights.astype(BF16)
            context = dot_nt(rounded, values)
            prob_grad = dot_nn(grad_rows, values)
            row_dot = jnp.sum(grad_rows.astype(F32) * context, axis=1, keepdims=True)
            dscore = (weights * (prob_grad - row_dot)).astype(BF16)
            query_grad = dot_nt(dscore, keys) * score_scale
            attended_ref[:, head * DL : (head + 1) * DL] = context.astype(BF16)
            dscore_ref[lane : lane + ROWS, :] = dscore
            prob_ref[lane : lane + ROWS, :] = rounded
            if odd:
                middle = before[:, DL:] + query_grad[:, : DK + PAD - DL]
                query_out_ref[:, left : left + DL] = before[:, :DL].astype(BF16)
                query_out_ref[:, left + DL : left + DK + PAD] = middle.astype(BF16)
                query_out_ref[:, left + DK + PAD : left + 2 * DK] = query_grad[:, DK + PAD - DL :].astype(BF16)
            before = query_grad

    dscore, rounded = dscore_ref[...], prob_ref[...]
    key_grad = dot_nn(query_t_ref[...], dscore) * score_scale
    value_grad = dot_nn(grad_t_ref[...], rounded)
    total = jnp.concatenate([key_grad[:DL] + value_grad, key_grad[DL:]], axis=0)
    for i, ref in enumerate((g4_ref, swap_out_ref.at[1], g2_ref, swap_out_ref.at[0], g0_ref)):
        ref[...] = total[:, i * ROWS : (i + 1) * ROWS].astype(ref.dtype)
    comp = dot_nt(picks, total[:, WKEYS:].astype(BF16))
    comp_out_ref[...] = comp.astype(BF16).reshape(comp_out_ref.shape)


def weight_kernel(comp_ref, own_ref, _r2_ref, _r4_ref, comp_out_ref, weight_out_ref):
    comp = jnp.sum(comp_ref[...].astype(F32), axis=0)
    comp_out_ref[...] = comp
    fold = (iota((CS, ROWS), 1) % CS == iota((CS, ROWS), 0)).astype(F32)
    wide = dot_tn(comp, owner(), **EXACT)
    part = dot_nt(fold, wide * own_ref[...].astype(F32), **EXACT).astype(BF16)
    for i in range(weight_out_ref.shape[0]):
        weight_out_ref[i] = part[OWN * i : OWN * (i + 1)]


def latent_kernel(place_ref, comp_ref, weight_ref, swap_ref, g0_ref, r2_ref, r4_ref, out_ref):
    wide = dot_tn(comp_ref[...], owner(), **EXACT)
    near = jnp.where(place_ref[0] % 2 == 0, swap_ref[0].astype(F32), 0.0)
    total = g0_ref[...] + near + r2_ref[...].astype(F32) + r4_ref[...].astype(F32)
    out_ref[...] = total + wide * spread_weight(weight_ref[...])


def sum_kernel(part_ref, out_ref):
    total = jnp.sum(part_ref[...].astype(F32), axis=0, keepdims=True)
    out_ref[...] = jnp.broadcast_to(total, out_ref.shape).astype(out_ref.dtype)


def call(kernel, outs, in_specs, *args, scratch=(), flops=0, mib=8):
    shapes = [jax.ShapeDtypeStruct(shape, dtype) for shape, dtype in outs]
    nbytes = sum(a.size * a.dtype.itemsize for a in args) + sum(s.size * s.dtype.itemsize for s in shapes)
    return pl.pallas_call(
        kernel,
        out_shape=shapes,
        in_specs=in_specs,
        out_specs=[VMEM] * len(shapes),
        scratch_shapes=scratch,
        compiler_params=pltpu.CompilerParams(vmem_limit_bytes=mib << 20),
        cost_estimate=pl.CostEstimate(flops=flops, bytes_accessed=nbytes, transcendentals=0),
    )(*args)


def attend(place, chosen, w4, w2, swap, own, gathered, query_rows, grad_rows):
    seg = (DK, ROWS)
    rows = H * ROWS
    return call(
        attend_kernel,
        [((ROWS, H * DL), BF16), ((ROWS, H * DK), BF16), ((PEERS, OWN, DK), BF16)]
        + [((2, *seg), BF16)] + [(seg, F32)] * 3,
        [SMEM] + [VMEM] * 8,
        place, chosen, w4, w2, swap, own, gathered, query_rows, grad_rows,
        scratch=[
            pltpu.VMEM((DK + 2 * PAD, KEYS), BF16),
            pltpu.VMEM((DK, rows), BF16),
            pltpu.VMEM((DL, rows), BF16),
            pltpu.VMEM((rows, KEYS), BF16),
            pltpu.VMEM((rows, KEYS), BF16),
        ],
        flops=2 * rows * KEYS * 6 * DK,
        mib=32,
    )


def shifted(block, distance):
    devices = range(PEERS)
    route = [(i - distance, i) for i in devices if i - distance in devices]
    return lax.ppermute(block, SEQ, route)


def swapped(block):
    return lax.ppermute(block, "c", [(0, 1), (1, 0)])


def exchange(pieces, axis):
    return lax.all_to_all(pieces, axis, 0, 0, tiled=True)


def body(queries, latents, cotangent, comp_weight, sel_idx, sel_count):
    own = latents[0].T
    place = lax.axis_index(SEQ).astype(jnp.int32).reshape(1)
    slots = jnp.arange(SEL, dtype=jnp.int32)
    chosen = jnp.where(slots[None, :] < sel_count[0][:, None], sel_idx[0], -1).reshape(1, 2 * SEL)
    seg = (DK, ROWS)
    pair = ((2, *seg), BF16)
    w2, w4 = shifted(own, 2), shifted(own, 4)
    (pieces,) = call(compress_kernel, [((PEERS, OWN, DK), BF16)], [VMEM] * 2, own, comp_weight)
    gathered = exchange(pieces, SEQ)
    (packed,) = call(pack_kernel, [pair], [SMEM] + [VMEM] * 3, place, own, w2, w4)
    attended, query_out, comp_pieces, swap_out, g4, g2, g0 = attend(
        place, chosen, w4, w2, swapped(packed), own, gathered, queries[0], cotangent[0]
    )
    comp_parts = exchange(comp_pieces, SEQ)
    swap_in = swapped(swap_out)
    send2, send4 = call(merge_kernel, [(seg, BF16)] * 2, [SMEM] + [VMEM] * 3, place, swap_in, g2, g4)
    r2, r4 = shifted(send2, -2), shifted(send4, -4)
    comp, part = call(
        weight_kernel,
        [((OWN, DK), F32), ((8, OWN, DK), BF16)],
        [VMEM] * 2 + [ANY] * 2,
        comp_parts, own, r2, r4,
    )
    for axis in (ROW, "y", "z"):
        (part,) = call(sum_kernel, [((8, OWN, DK), BF16)], [VMEM], exchange(part, axis))
    weight_grad = exchange(part, ROW).reshape(CS, DK).astype(F32)
    (latent_grad,) = call(
        latent_kernel, [(seg, F32)], [SMEM] + [VMEM] * 6, place, comp, comp_weight, swap_in, g0, r2, r4
    )
    return (attended[None], query_out[None], latent_grad.T[None], weight_grad)


def solution(mesh):
    torus = Mesh(mesh.devices.reshape(mesh.shape["grp"], -1, 4, 2), ("z", "y", "x", "c"))
    split = P("z", SEQ, None)
    in_specs = (split, split, split, P(), split, P("z", SEQ))
    out_specs = (split, split, split, P())
    return jax.shard_map(body, mesh=torus, in_specs=in_specs, out_specs=out_specs, check_vma=False)
```

```python
import jax
import jax.numpy as jnp
from jax import lax
from jax.experimental import pallas as pl
from jax.experimental.pallas import tpu as pltpu
from jax.sharding import Mesh, PartitionSpec as P

DL = 512
DR = 64
H = 8
QB = 64
CS = 32
SEL = 64
WIN = 512
DK = 576

ROWS = 128
OWN = ROWS // CS
PEERS = 64
WKEYS = WIN + ROWS
KEYS = WKEYS + 2 * SEL
PAD = DR

SEQ = ("y", "x", "c")
ROW = ("x", "c")

score_scale = 192.0 ** (-0.5)
F32 = jnp.float32
BF16 = jnp.bfloat16
VMEM = pl.BlockSpec(memory_space=pltpu.VMEM)
SMEM = pl.BlockSpec(memory_space=pltpu.SMEM)


def iota(shape, dim):
    return lax.broadcasted_iota(jnp.int32, shape, dim)


def dot_nn(a, b, **kw):
    return lax.dot_general(a, b, (((1,), (0,)), ((), ())), preferred_element_type=F32, **kw)


def dot_nt(a, b, **kw):
    return lax.dot_general(a, b, (((1,), (1,)), ((), ())), preferred_element_type=F32, **kw)


def dot_tn(a, b, **kw):
    return lax.dot_general(a, b, (((0,), (0,)), ((), ())), preferred_element_type=F32, **kw)


EXACT = dict(precision=lax.Precision.HIGHEST)


def spread_weight(weight):
    return dot_tn(weight, (iota((CS, ROWS), 1) % CS == iota((CS, ROWS), 0)).astype(F32), **EXACT)


def owner():
    return (iota((OWN, ROWS), 1) // CS == iota((OWN, ROWS), 0)).astype(F32)


def compress_kernel(own_ref, weight_ref, out_ref):
    terms = own_ref[...].astype(F32) * spread_weight(weight_ref[...])
    piece = dot_nt(owner(), terms, **EXACT)
    out_ref[...] = jnp.broadcast_to(piece.astype(BF16)[None], out_ref.shape)


def pack_kernel(place_ref, own_ref, w2_ref, w4_ref, out_ref):
    first = place_ref[0] % 2 == 0
    w2 = w2_ref[...]
    out_ref[0] = jnp.where(first, w2, w4_ref[...])
    out_ref[1] = jnp.where(first, own_ref[...], w2)


def merge_kernel(place_ref, swap_ref, g2_ref, g4_ref, out2_ref, out4_ref):
    first = place_ref[0] % 2 == 0
    near, far = swap_ref[0].astype(F32), swap_ref[1].astype(F32)
    out2_ref[...] = (g2_ref[...] + jnp.where(first, far, near)).astype(BF16)
    out4_ref[...] = (g4_ref[...] + jnp.where(first, 0.0, far)).astype(BF16)


def attend_kernel(
    place_ref, chosen_ref, w4_ref, w2_ref, swap_ref, own_ref, comp_ref, query_ref, grad_ref,
    attended_ref, query_out_ref, comp_out_ref, swap_out_ref, g4_ref, g2_ref, g0_ref,
    key_ref, query_t_ref, grad_t_ref, dscore_ref, prob_ref,
):
    place = place_ref[0]
    chosen = chosen_ref[...]
    key_ref[:PAD, :] = jnp.zeros((PAD, KEYS), BF16)
    key_ref[PAD + DK :, :] = jnp.zeros((PAD, KEYS), BF16)
    for i, ref in enumerate((w4_ref, swap_ref.at[0], w2_ref, swap_ref.at[1], own_ref)):
        key_ref[PAD : PAD + DK, i * ROWS : (i + 1) * ROWS] = ref[...]
    picks = (iota((OWN * PEERS, 2 * SEL), 0) == chosen).astype(F32).astype(BF16)
    pieces = comp_ref[...].reshape(OWN * PEERS, DK)
    key_ref[PAD : PAD + DK, WKEYS:] = dot_tn(pieces, picks).astype(BF16)

    token = iota((ROWS, KEYS), 0)
    key = iota((ROWS, KEYS), 1)
    near = (key <= token + WIN) & (key > token) & (key >= WIN - place * ROWS)
    picked = (key - WKEYS) // SEL == token // QB
    live = jnp.broadcast_to(chosen >= 0, (ROWS, 2 * SEL))
    live = jnp.concatenate([jnp.zeros((ROWS, WKEYS), jnp.int32), live.astype(jnp.int32)], axis=1) > 0
    allowed = jnp.where(key < WKEYS, near.astype(jnp.int32), (picked & live).astype(jnp.int32)) > 0
    values = key_ref[PAD : PAD + DL, :]

    for pair in range(H // 2):
        left = pair * 2 * DK
        query_pair = query_ref[:, left : left + 2 * DK]
        query_pair_t = query_pair.T
        for odd in range(2):
            head = 2 * pair + odd
            lane = head * ROWS
            query_t_ref[:, lane : lane + ROWS] = query_pair_t[odd * DK : (odd + 1) * DK]
            grad_rows = grad_ref[:, head * DL : (head + 1) * DL]
            grad_t_ref[:, lane : lane + ROWS] = grad_rows.T
            keys = key_ref[:DK + PAD, :] if odd else key_ref[PAD:, :]
            query_rows = query_pair[:, DL:] if odd else query_pair[:, : DK + PAD]
            scores = jnp.where(allowed, dot_nn(query_rows, keys) * score_scale, -1e30)
            expo = jnp.exp(scores - jnp.max(scores, axis=1, keepdims=True))
            weights = expo * (1.0 / jnp.sum(expo, axis=1, keepdims=True))
            rounded = weights.astype(BF16)
            context = dot_nt(rounded, values)
            prob_grad = dot_nn(grad_rows, values)
            row_dot = jnp.sum(grad_rows.astype(F32) * context, axis=1, keepdims=True)
            dscore = (weights * (prob_grad - row_dot)).astype(BF16)
            query_grad = dot_nt(dscore, keys) * score_scale
            attended_ref[:, head * DL : (head + 1) * DL] = context.astype(BF16)
            dscore_ref[lane : lane + ROWS, :] = dscore
            prob_ref[lane : lane + ROWS, :] = rounded
            if odd:
                middle = before[:, DL:] + query_grad[:, : DK + PAD - DL]
                query_out_ref[:, left : left + DL] = before[:, :DL].astype(BF16)
                query_out_ref[:, left + DL : left + DK + PAD] = middle.astype(BF16)
                query_out_ref[:, left + DK + PAD : left + 2 * DK] = query_grad[:, DK + PAD - DL :].astype(BF16)
            before = query_grad

    dscore, rounded = dscore_ref[...], prob_ref[...]
    key_grad = dot_nn(query_t_ref[...], dscore) * score_scale
    value_grad = dot_nn(grad_t_ref[...], rounded)
    total = jnp.concatenate([key_grad[:DL] + value_grad, key_grad[DL:]], axis=0)
    for i, ref in enumerate((g4_ref, swap_out_ref.at[1], g2_ref, swap_out_ref.at[0], g0_ref)):
        ref[...] = total[:, i * ROWS : (i + 1) * ROWS].astype(ref.dtype)
    comp = dot_nt(picks, total[:, WKEYS:].astype(BF16))
    comp_out_ref[...] = comp.astype(BF16).reshape(comp_out_ref.shape)


def weight_kernel(comp_ref, own_ref, comp_out_ref, weight_out_ref):
    comp = jnp.sum(comp_ref[...].astype(F32), axis=0)
    comp_out_ref[...] = comp
    fold = (iota((CS, ROWS), 1) % CS == iota((CS, ROWS), 0)).astype(F32)
    wide = dot_tn(comp, owner(), **EXACT)
    part = dot_nt(fold, wide * own_ref[...].astype(F32), **EXACT).astype(BF16)
    for i in range(weight_out_ref.shape[0]):
        weight_out_ref[i] = part[OWN * i : OWN * (i + 1)]


def latent_kernel(place_ref, comp_ref, weight_ref, swap_ref, g0_ref, r2_ref, r4_ref, out_ref):
    wide = dot_tn(comp_ref[...], owner(), **EXACT)
    near = jnp.where(place_ref[0] % 2 == 0, swap_ref[0].astype(F32), 0.0)
    total = g0_ref[...] + near + r2_ref[...].astype(F32) + r4_ref[...].astype(F32)
    out_ref[...] = total + wide * spread_weight(weight_ref[...])


def sum_kernel(part_ref, out_ref):
    total = jnp.sum(part_ref[...].astype(F32), axis=0, keepdims=True)
    out_ref[...] = jnp.broadcast_to(total, out_ref.shape).astype(out_ref.dtype)


def call(kernel, outs, in_specs, *args, scratch=(), flops=0, mib=8):
    shapes = [jax.ShapeDtypeStruct(shape, dtype) for shape, dtype in outs]
    nbytes = sum(a.size * a.dtype.itemsize for a in args) + sum(s.size * s.dtype.itemsize for s in shapes)
    return pl.pallas_call(
        kernel,
        out_shape=shapes,
        in_specs=in_specs,
        out_specs=[VMEM] * len(shapes),
        scratch_shapes=scratch,
        compiler_params=pltpu.CompilerParams(vmem_limit_bytes=mib << 20),
        cost_estimate=pl.CostEstimate(flops=flops, bytes_accessed=nbytes, transcendentals=0),
    )(*args)


def attend(place, chosen, w4, w2, swap, own, gathered, query_rows, grad_rows):
    seg = (DK, ROWS)
    rows = H * ROWS
    return call(
        attend_kernel,
        [((ROWS, H * DL), BF16), ((ROWS, H * DK), BF16), ((PEERS, OWN, DK), BF16)]
        + [((2, *seg), BF16)] + [(seg, F32)] * 3,
        [SMEM] + [VMEM] * 8,
        place, chosen, w4, w2, swap, own, gathered, query_rows, grad_rows,
        scratch=[
            pltpu.VMEM((DK + 2 * PAD, KEYS), BF16),
            pltpu.VMEM((DK, rows), BF16),
            pltpu.VMEM((DL, rows), BF16),
            pltpu.VMEM((rows, KEYS), BF16),
            pltpu.VMEM((rows, KEYS), BF16),
        ],
        flops=2 * rows * KEYS * 6 * DK,
        mib=32,
    )


def shifted(block, distance):
    devices = range(PEERS)
    route = [(i - distance, i) for i in devices if i - distance in devices]
    return lax.ppermute(block, SEQ, route)


def swapped(block):
    return lax.ppermute(block, "c", [(0, 1), (1, 0)])


def exchange(pieces, axis):
    return lax.all_to_all(pieces, axis, 0, 0, tiled=True)


def step(queries, latents, cotangent, comp_weight, sel_idx, sel_count):
    own = latents[0].T
    place = lax.axis_index(SEQ).astype(jnp.int32).reshape(1)
    slots = jnp.arange(SEL, dtype=jnp.int32)
    chosen = jnp.where(slots[None, :] < sel_count[0][:, None], sel_idx[0], -1).reshape(1, 2 * SEL)
    seg = (DK, ROWS)
    pair = ((2, *seg), BF16)
    w2 = shifted(own, 2)
    w4 = shifted(own, 4)
    (pieces,) = call(compress_kernel, [((PEERS, OWN, DK), BF16)], [VMEM] * 2, own, comp_weight, mib=56)
    gathered = exchange(pieces, SEQ)
    (packed,) = call(pack_kernel, [pair], [SMEM] + [VMEM] * 3, place, own, w2, w4)
    attended, query_out, comp_pieces, swap_out, g4, g2, g0 = attend(
        place, chosen, w4, w2, swapped(packed), own, gathered, queries[0], cotangent[0]
    )
    comp_parts = exchange(comp_pieces, SEQ)
    swap_in = swapped(swap_out)
    send2, send4 = call(merge_kernel, [(seg, BF16)] * 2, [SMEM] + [VMEM] * 3, place, swap_in, g2, g4)
    r2, r4 = shifted(send2, -2), shifted(send4, -4)
    comp, part = call(
        weight_kernel, [((OWN, DK), F32), ((8, OWN, DK), BF16)], [VMEM] * 2, comp_parts, own
    )
    for axis in (ROW, "y", "z"):
        (part,) = call(sum_kernel, [((8, OWN, DK), BF16)], [VMEM], exchange(part, axis))
    weight_grad = exchange(part, ROW).reshape(CS, DK).astype(F32)
    (latent_grad,) = call(
        latent_kernel, [(seg, F32)], [SMEM] + [VMEM] * 6, place, comp, comp_weight, swap_in, g0, r2, r4
    )
    return (attended[None], query_out[None], latent_grad.T[None], weight_grad)


def solution(mesh):
    torus = Mesh(mesh.devices.reshape(mesh.shape["grp"], -1, 4, 2), ("z", "y", "x", "c"))
    split = P("z", SEQ, None)
    in_specs = (split, split, split, P(), split, P("z", SEQ))
    out_specs = (split, split, split, P())
    return jax.shard_map(step, mesh=torus, in_specs=in_specs, out_specs=out_specs, check_vma=False)
```

```python
import jax
import jax.numpy as jnp
from jax import lax
from jax.experimental import pallas as pl
from jax.experimental.pallas import tpu as pltpu
from jax.sharding import Mesh, PartitionSpec as P

DL = 512
DR = 64
H = 8
QB = 64
CS = 32
SEL = 64
WIN = 512
DK = 576

ROWS = 128
OWN = ROWS // CS
PEERS = 64
WKEYS = WIN + ROWS
KEYS = WKEYS + 2 * SEL
PAD = DR

SEQ = ("y", "x", "c")
ROW = ("x", "c")

score_scale = 192.0 ** (-0.5)
F32 = jnp.float32
BF16 = jnp.bfloat16
VMEM = pl.BlockSpec(memory_space=pltpu.VMEM)
SMEM = pl.BlockSpec(memory_space=pltpu.SMEM)


def iota(shape, dim):
    return lax.broadcasted_iota(jnp.int32, shape, dim)


def dot_nn(a, b, **kw):
    return lax.dot_general(a, b, (((1,), (0,)), ((), ())), preferred_element_type=F32, **kw)


def dot_nt(a, b, **kw):
    return lax.dot_general(a, b, (((1,), (1,)), ((), ())), preferred_element_type=F32, **kw)


def dot_tn(a, b, **kw):
    return lax.dot_general(a, b, (((0,), (0,)), ((), ())), preferred_element_type=F32, **kw)


EXACT = dict(precision=lax.Precision.HIGHEST)


def spread_weight(weight):
    return dot_tn(weight, (iota((CS, ROWS), 1) % CS == iota((CS, ROWS), 0)).astype(F32), **EXACT)


def owner():
    return (iota((OWN, ROWS), 1) // CS == iota((OWN, ROWS), 0)).astype(F32)


def compress_kernel(own_ref, weight_ref, out_ref):
    terms = own_ref[...].astype(F32) * spread_weight(weight_ref[...])
    piece = dot_nt(owner(), terms, **EXACT)
    out_ref[...] = jnp.broadcast_to(piece.astype(BF16)[None], out_ref.shape)


def pack_kernel(place_ref, own_ref, w2_ref, w4_ref, out_ref):
    first = place_ref[0] % 2 == 0
    w2 = w2_ref[...]
    out_ref[0] = jnp.where(first, w2, w4_ref[...])
    out_ref[1] = jnp.where(first, own_ref[...], w2)


def merge_kernel(place_ref, swap_ref, g2_ref, g4_ref, out2_ref, out4_ref):
    first = place_ref[0] % 2 == 0
    near, far = swap_ref[0].astype(F32), swap_ref[1].astype(F32)
    out2_ref[...] = (g2_ref[...] + jnp.where(first, far, near)).astype(BF16)
    out4_ref[...] = (g4_ref[...] + jnp.where(first, 0.0, far)).astype(BF16)


def attend_kernel(
    place_ref, chosen_ref, w4_ref, w2_ref, swap_ref, own_ref, comp_ref, query_ref, grad_ref,
    attended_ref, query_out_ref, comp_out_ref, swap_out_ref, g4_ref, g2_ref, g0_ref,
    key_ref, query_t_ref, grad_t_ref, dscore_ref, prob_ref, bias_ref,
):
    place = place_ref[0]
    chosen = chosen_ref[...]
    key_ref[:PAD, :] = jnp.zeros((PAD, KEYS), BF16)
    key_ref[PAD + DK :, :] = jnp.zeros((PAD, KEYS), BF16)
    for i, ref in enumerate((w4_ref, swap_ref.at[0], w2_ref, swap_ref.at[1], own_ref)):
        key_ref[PAD : PAD + DK, i * ROWS : (i + 1) * ROWS] = ref[...]
    picks = (iota((OWN * PEERS, 2 * SEL), 0) == chosen).astype(F32).astype(BF16)
    pieces = comp_ref[...].reshape(OWN * PEERS, DK)
    key_ref[PAD : PAD + DK, WKEYS:] = dot_tn(pieces, picks).astype(BF16)

    heads = H // 2
    token = iota((heads * ROWS, KEYS), 0) % ROWS
    key = iota((heads * ROWS, KEYS), 1)
    near = (key <= token + WIN) & (key > token) & (key >= WIN - place * ROWS)
    picked = (key - WKEYS) // SEL == token // QB
    live = jnp.concatenate([jnp.zeros((1, WKEYS), jnp.int32), (chosen >= 0).astype(jnp.int32)], axis=1)
    live = jnp.broadcast_to(live, (heads * ROWS, KEYS)) > 0
    allowed = jnp.where(key < WKEYS, near.astype(jnp.int32), (picked & live).astype(jnp.int32)) > 0
    bias_ref[...] = jnp.where(allowed, 0.0, -1e30)
    values = key_ref[PAD : PAD + DL, :]

    for pair in range(heads):
        left = pair * 2 * DK
        query_pair_t = query_ref[:, left : left + 2 * DK].T
        for odd in range(2):
            lane = (odd * heads + pair) * ROWS
            query_t_ref[:, lane : lane + ROWS] = query_pair_t[odd * DK : (odd + 1) * DK]
            head = 2 * pair + odd
            grad_t_ref[:, lane : lane + ROWS] = grad_ref[:, head * DL : (head + 1) * DL].T
    grads = []
    for odd in range(2):
        rows = slice(odd * heads * ROWS, (odd + 1) * heads * ROWS)
        keys = key_ref[:DK + PAD, :] if odd else key_ref[PAD:, :]
        starts = [(2 * pair * DK) + odd * DL for pair in range(heads)]
        query_rows = jnp.concatenate([query_ref[:, a : a + DK + PAD] for a in starts], axis=0)
        starts = [(2 * pair + odd) * DL for pair in range(heads)]
        grad_rows = jnp.concatenate([grad_ref[:, a : a + DL] for a in starts], axis=0)
        scores = dot_nn(query_rows, keys) * score_scale + bias_ref[...]
        expo = jnp.exp(scores - jnp.max(scores, axis=1, keepdims=True))
        weights = expo * (1.0 / jnp.sum(expo, axis=1, keepdims=True))
        rounded = weights.astype(BF16)
        prob_ref[rows, :] = rounded
        context = dot_nt(rounded, values)
        prob_grad = dot_nn(grad_rows, values)
        row_dot = jnp.sum(grad_rows.astype(F32) * context, axis=1, keepdims=True)
        dscore = (weights * (prob_grad - row_dot)).astype(BF16)
        dscore_ref[rows, :] = dscore
        grads.append(dot_nt(dscore, keys) * score_scale)
        for pair in range(heads):
            a = starts[pair]
            attended_ref[:, a : a + DL] = context[pair * ROWS : (pair + 1) * ROWS].astype(BF16)
    for pair in range(heads):
        left = pair * 2 * DK
        even, odd = (g[pair * ROWS : (pair + 1) * ROWS] for g in grads)
        middle = even[:, DL:] + odd[:, : DK + PAD - DL]
        query_out_ref[:, left : left + DL] = even[:, :DL].astype(BF16)
        query_out_ref[:, left + DL : left + DK + PAD] = middle.astype(BF16)
        query_out_ref[:, left + DK + PAD : left + 2 * DK] = odd[:, DK + PAD - DL :].astype(BF16)

    dscore, rounded = dscore_ref[...], prob_ref[...]
    key_grad = dot_nn(query_t_ref[...], dscore) * score_scale
    value_grad = dot_nn(grad_t_ref[...], rounded)
    total = jnp.concatenate([key_grad[:DL] + value_grad, key_grad[DL:]], axis=0)
    for i, ref in enumerate((g4_ref, swap_out_ref.at[1], g2_ref, swap_out_ref.at[0], g0_ref)):
        ref[...] = total[:, i * ROWS : (i + 1) * ROWS].astype(ref.dtype)
    comp = dot_nt(picks, total[:, WKEYS:].astype(BF16))
    comp_out_ref[...] = comp.astype(BF16).reshape(comp_out_ref.shape)


def weight_kernel(comp_ref, own_ref, comp_out_ref, weight_out_ref):
    comp = jnp.sum(comp_ref[...].astype(F32), axis=0)
    comp_out_ref[...] = comp
    fold = (iota((CS, ROWS), 1) % CS == iota((CS, ROWS), 0)).astype(F32)
    wide = dot_tn(comp, owner(), **EXACT)
    part = dot_nt(fold, wide * own_ref[...].astype(F32), **EXACT).astype(BF16)
    for i in range(weight_out_ref.shape[0]):
        weight_out_ref[i] = part[OWN * i : OWN * (i + 1)]


def latent_kernel(place_ref, comp_ref, weight_ref, swap_ref, g0_ref, r2_ref, r4_ref, out_ref):
    wide = dot_tn(comp_ref[...], owner(), **EXACT)
    near = jnp.where(place_ref[0] % 2 == 0, swap_ref[0].astype(F32), 0.0)
    total = g0_ref[...] + near + r2_ref[...].astype(F32) + r4_ref[...].astype(F32)
    out_ref[...] = total + wide * spread_weight(weight_ref[...])


def sum_kernel(part_ref, out_ref):
    total = jnp.sum(part_ref[...].astype(F32), axis=0, keepdims=True)
    out_ref[...] = jnp.broadcast_to(total, out_ref.shape).astype(out_ref.dtype)


def call(kernel, outs, in_specs, *args, scratch=(), flops=0, mib=8):
    shapes = [jax.ShapeDtypeStruct(shape, dtype) for shape, dtype in outs]
    nbytes = sum(a.size * a.dtype.itemsize for a in args) + sum(s.size * s.dtype.itemsize for s in shapes)
    return pl.pallas_call(
        kernel,
        out_shape=shapes,
        in_specs=in_specs,
        out_specs=[VMEM] * len(shapes),
        scratch_shapes=scratch,
        compiler_params=pltpu.CompilerParams(vmem_limit_bytes=mib << 20),
        cost_estimate=pl.CostEstimate(flops=flops, bytes_accessed=nbytes, transcendentals=0),
    )(*args)


def attend(place, chosen, w4, w2, swap, own, gathered, query_rows, grad_rows):
    seg = (DK, ROWS)
    rows = H * ROWS
    return call(
        attend_kernel,
        [((ROWS, H * DL), BF16), ((ROWS, H * DK), BF16), ((PEERS, OWN, DK), BF16)]
        + [((2, *seg), BF16)] + [(seg, F32)] * 3,
        [SMEM] + [VMEM] * 8,
        place, chosen, w4, w2, swap, own, gathered, query_rows, grad_rows,
        scratch=[
            pltpu.VMEM((DK + 2 * PAD, KEYS), BF16),
            pltpu.VMEM((DK, rows), BF16),
            pltpu.VMEM((DL, rows), BF16),
            pltpu.VMEM((rows, KEYS), BF16),
            pltpu.VMEM((rows, KEYS), BF16),
            pltpu.VMEM((rows // 2, KEYS), F32),
        ],
        flops=2 * rows * KEYS * 6 * DK,
        mib=40,
    )


def shifted(block, distance):
    devices = range(PEERS)
    route = [(i - distance, i) for i in devices if i - distance in devices]
    return lax.ppermute(block, SEQ, route)


def swapped(block):
    return lax.ppermute(block, "c", [(0, 1), (1, 0)])


def exchange(pieces, axis):
    return lax.all_to_all(pieces, axis, 0, 0, tiled=True)


def step(queries, latents, cotangent, comp_weight, sel_idx, sel_count):
    own = latents[0].T
    place = lax.axis_index(SEQ).astype(jnp.int32).reshape(1)
    slots = jnp.arange(SEL, dtype=jnp.int32)
    chosen = jnp.where(slots[None, :] < sel_count[0][:, None], sel_idx[0], -1).reshape(1, 2 * SEL)
    seg = (DK, ROWS)
    pair = ((2, *seg), BF16)
    w2 = shifted(own, 2)
    w4 = shifted(own, 4)
    (pieces,) = call(compress_kernel, [((PEERS, OWN, DK), BF16)], [VMEM] * 2, own, comp_weight, mib=56)
    gathered = exchange(pieces, SEQ)
    (packed,) = call(pack_kernel, [pair], [SMEM] + [VMEM] * 3, place, own, w2, w4)
    attended, query_out, comp_pieces, swap_out, g4, g2, g0 = attend(
        place, chosen, w4, w2, swapped(packed), own, gathered, queries[0], cotangent[0]
    )
    comp_parts = exchange(comp_pieces, SEQ)
    swap_in = swapped(swap_out)
    send2, send4 = call(merge_kernel, [(seg, BF16)] * 2, [SMEM] + [VMEM] * 3, place, swap_in, g2, g4)
    r2, r4 = shifted(send2, -2), shifted(send4, -4)
    comp, part = call(
        weight_kernel, [((OWN, DK), F32), ((8, OWN, DK), BF16)], [VMEM] * 2, comp_parts, own
    )
    for axis in (ROW, "y", "z"):
        (part,) = call(sum_kernel, [((8, OWN, DK), BF16)], [VMEM], exchange(part, axis))
    weight_grad = exchange(part, ROW).reshape(CS, DK).astype(F32)
    (latent_grad,) = call(
        latent_kernel, [(seg, F32)], [SMEM] + [VMEM] * 6, place, comp, comp_weight, swap_in, g0, r2, r4
    )
    return (attended[None], query_out[None], latent_grad.T[None], weight_grad)


def solution(mesh):
    torus = Mesh(mesh.devices.reshape(mesh.shape["grp"], -1, 4, 2), ("z", "y", "x", "c"))
    split = P("z", SEQ, None)
    in_specs = (split, split, split, P(), split, P("z", SEQ))
    out_specs = (split, split, split, P())
    return jax.shard_map(step, mesh=torus, in_specs=in_specs, out_specs=out_specs, check_vma=False)
```

```python
import jax
import jax.numpy as jnp
from jax import lax
from jax.experimental import pallas as pl
from jax.experimental.pallas import tpu as pltpu
from jax.sharding import Mesh, PartitionSpec as P

DL = 512
DR = 64
H = 8
QB = 64
CS = 32
SEL = 64
WIN = 512
DK = 576

ROWS = 128
OWN = ROWS // CS
PEERS = 64
WKEYS = WIN + ROWS
KEYS = WKEYS + 2 * SEL
MIB = 28
PAD = DR

SEQ = ("y", "x", "c")
ROW = ("x", "c")

score_scale = 192.0 ** (-0.5)
F32 = jnp.float32
BF16 = jnp.bfloat16
VMEM = pl.BlockSpec(memory_space=pltpu.VMEM)
SMEM = pl.BlockSpec(memory_space=pltpu.SMEM)


def iota(shape, dim):
    return lax.broadcasted_iota(jnp.int32, shape, dim)


def dot_nn(a, b, **kw):
    return lax.dot_general(a, b, (((1,), (0,)), ((), ())), preferred_element_type=F32, **kw)


def dot_nt(a, b, **kw):
    return lax.dot_general(a, b, (((1,), (1,)), ((), ())), preferred_element_type=F32, **kw)


def dot_tn(a, b, **kw):
    return lax.dot_general(a, b, (((0,), (0,)), ((), ())), preferred_element_type=F32, **kw)


EXACT = dict(precision=lax.Precision.HIGHEST)


def spread_weight(weight):
    return dot_tn(weight, (iota((CS, ROWS), 1) % CS == iota((CS, ROWS), 0)).astype(F32), **EXACT)


def owner():
    return (iota((OWN, ROWS), 1) // CS == iota((OWN, ROWS), 0)).astype(F32)


def compress_kernel(own_ref, weight_ref, out_ref):
    terms = own_ref[...].astype(F32) * spread_weight(weight_ref[...])
    piece = dot_nt(owner(), terms, **EXACT)
    out_ref[...] = jnp.broadcast_to(piece.astype(BF16)[None], out_ref.shape)


def pack_kernel(place_ref, own_ref, w2_ref, w4_ref, out_ref):
    first = place_ref[0] % 2 == 0
    w2 = w2_ref[...]
    out_ref[0] = jnp.where(first, w2, w4_ref[...])
    out_ref[1] = jnp.where(first, own_ref[...], w2)


def merge_kernel(place_ref, swap_ref, g2_ref, g4_ref, out2_ref, out4_ref):
    first = place_ref[0] % 2 == 0
    near, far = swap_ref[0].astype(F32), swap_ref[1].astype(F32)
    out2_ref[...] = (g2_ref[...] + jnp.where(first, far, near)).astype(BF16)
    out4_ref[...] = (g4_ref[...] + jnp.where(first, 0.0, far)).astype(BF16)


def stack_kernel(query_ref, grad_ref, query_out_ref, grad_out_ref, query_t_ref, grad_t_ref):
    for pair in range(H // 2):
        query_pair_t = query_ref[:, pair * 2 * DK : (pair + 1) * 2 * DK].T
        for odd in range(2):
            head = 2 * pair + odd
            rows = slice((odd * H // 2 + pair) * ROWS, (odd * H // 2 + pair + 1) * ROWS)
            start = pair * 2 * DK + odd * DL
            query_out_ref[rows, :] = query_ref[:, start : start + DK + PAD]
            query_t_ref[:, rows] = query_pair_t[odd * DK : (odd + 1) * DK]
            grad_rows = grad_ref[:, head * DL : (head + 1) * DL]
            grad_out_ref[rows, :] = grad_rows
            grad_t_ref[:, rows] = grad_rows.T


def attend_kernel(
    place_ref, count_ref, index_ref, w4_ref, w2_ref, swap_ref, own_ref, mine_ref, mates_ref, query_ref, grad_ref, query_t_ref, grad_t_ref,
    attended_ref, query_out_ref, comp_out_ref, swap_out_ref, g4_ref, g2_ref, g0_ref,
    key_ref, dscore_ref, prob_ref, bias_ref,
):
    place = place_ref[0]
    slot = iota((1, SEL), 1)
    chosen = [jnp.where(slot < count_ref[0, r], index_ref[r : r + 1, :], -1) for r in range(2)]
    chosen = jnp.concatenate(chosen, axis=1)
    key_ref[:PAD, :] = jnp.zeros((PAD, KEYS), BF16)
    key_ref[PAD + DK :, :] = jnp.zeros((PAD, KEYS), BF16)
    for i, ref in enumerate((w4_ref, swap_ref.at[0], w2_ref, swap_ref.at[1], own_ref)):
        key_ref[PAD : PAD + DK, i * ROWS : (i + 1) * ROWS] = ref[...]
    picks = (iota((OWN * PEERS, 2 * SEL), 0) == chosen).astype(F32).astype(BF16)
    row = iota((OWN * PEERS // 2, 2 * SEL), 0)
    picked_keys = jnp.zeros((DK, 2 * SEL), F32)
    for ref, core in ((mine_ref, place % 2), (mates_ref, 1 - place % 2)):
        picks_here = (2 * OWN * (row // OWN) + row % OWN + OWN * core == chosen).astype(F32).astype(BF16)
        picked_keys = picked_keys + dot_tn(ref[...].reshape(OWN * PEERS // 2, DK), picks_here)
    key_ref[PAD : PAD + DK, WKEYS:] = picked_keys.astype(BF16)

    heads = H // 2
    token = iota((heads * ROWS, KEYS), 0) % ROWS
    key = iota((heads * ROWS, KEYS), 1)
    near = (key <= token + WIN) & (key > token) & (key >= WIN - place * ROWS)
    picked = (key - WKEYS) // SEL == token // QB
    live = jnp.concatenate([jnp.zeros((1, WKEYS), jnp.int32), (chosen >= 0).astype(jnp.int32)], axis=1)
    live = jnp.broadcast_to(live, (heads * ROWS, KEYS)) > 0
    allowed = jnp.where(key < WKEYS, near.astype(jnp.int32), (picked & live).astype(jnp.int32)) > 0
    bias_ref[...] = jnp.where(allowed, 0.0, -1e30)
    values = key_ref[PAD : PAD + DL, :]

    grads = []
    for odd in range(2):
        rows = slice(odd * heads * ROWS, (odd + 1) * heads * ROWS)
        keys = key_ref[:DK + PAD, :] if odd else key_ref[PAD:, :]
        query_rows, grad_rows = query_ref[rows, :], grad_ref[rows, :]
        scores = dot_nn(query_rows, keys) * score_scale + bias_ref[...]
        expo = jnp.exp(scores - jnp.max(scores, axis=1, keepdims=True))
        weights = expo * (1.0 / jnp.sum(expo, axis=1, keepdims=True))
        rounded = weights.astype(BF16)
        prob_ref[rows, :] = rounded
        context = dot_nt(rounded, values)
        prob_grad = dot_nn(grad_rows, values)
        row_dot = jnp.sum(grad_rows.astype(F32) * context, axis=1, keepdims=True)
        dscore = (weights * (prob_grad - row_dot)).astype(BF16)
        dscore_ref[rows, :] = dscore
        grads.append(dot_nt(dscore, keys) * score_scale)
        for pair in range(heads):
            a = (2 * pair + odd) * DL
            attended_ref[:, a : a + DL] = context[pair * ROWS : (pair + 1) * ROWS].astype(BF16)
    for pair in range(heads):
        left = pair * 2 * DK
        even, odd = (g[pair * ROWS : (pair + 1) * ROWS] for g in grads)
        middle = even[:, DL:] + odd[:, : DK + PAD - DL]
        query_out_ref[:, left : left + DL] = even[:, :DL].astype(BF16)
        query_out_ref[:, left + DL : left + DK + PAD] = middle.astype(BF16)
        query_out_ref[:, left + DK + PAD : left + 2 * DK] = odd[:, DK + PAD - DL :].astype(BF16)

    dscore, rounded = dscore_ref[...], prob_ref[...]
    key_grad = dot_nn(query_t_ref[...], dscore) * score_scale
    value_grad = dot_nn(grad_t_ref[...], rounded)
    total = jnp.concatenate([key_grad[:DL] + value_grad, key_grad[DL:]], axis=0)
    for i, ref in enumerate((g4_ref, swap_out_ref.at[1], g2_ref, swap_out_ref.at[0], g0_ref)):
        ref[...] = total[:, i * ROWS : (i + 1) * ROWS].astype(ref.dtype)
    comp = dot_nt(picks, total[:, WKEYS:].astype(BF16))
    comp_out_ref[...] = comp.astype(BF16).reshape(comp_out_ref.shape)


def weight_kernel(comp_ref, own_ref, comp_out_ref, weight_out_ref):
    comp = jnp.sum(comp_ref[...].astype(F32), axis=0)
    comp_out_ref[...] = comp
    fold = (iota((CS, ROWS), 1) % CS == iota((CS, ROWS), 0)).astype(F32)
    wide = dot_tn(comp, owner(), **EXACT)
    part = dot_nt(fold, wide * own_ref[...].astype(F32), **EXACT).astype(BF16)
    for i in range(weight_out_ref.shape[0]):
        weight_out_ref[i] = part[OWN * i : OWN * (i + 1)]


def latent_kernel(place_ref, comp_ref, weight_ref, swap_ref, g0_ref, r2_ref, r4_ref, out_ref):
    wide = dot_tn(comp_ref[...], owner(), **EXACT)
    near = jnp.where(place_ref[0] % 2 == 0, swap_ref[0].astype(F32), 0.0)
    total = g0_ref[...] + near + r2_ref[...].astype(F32) + r4_ref[...].astype(F32)
    out_ref[...] = total + wide * spread_weight(weight_ref[...])


def sum_kernel(part_ref, out_ref):
    total = jnp.sum(part_ref[...].astype(F32), axis=0, keepdims=True)
    out_ref[...] = jnp.broadcast_to(total, out_ref.shape).astype(out_ref.dtype)


def call(kernel, outs, in_specs, *args, scratch=(), flops=0, mib=8):
    shapes = [jax.ShapeDtypeStruct(shape, dtype) for shape, dtype in outs]
    nbytes = sum(a.size * a.dtype.itemsize for a in args) + sum(s.size * s.dtype.itemsize for s in shapes)
    return pl.pallas_call(
        kernel,
        out_shape=shapes,
        in_specs=in_specs,
        out_specs=[VMEM] * len(shapes),
        scratch_shapes=scratch,
        compiler_params=pltpu.CompilerParams(vmem_limit_bytes=mib << 20),
        cost_estimate=pl.CostEstimate(flops=flops, bytes_accessed=nbytes, transcendentals=0),
    )(*args)


def attend(place, count, index, w4, w2, swap, own, mine, mates, stacked):
    seg = (DK, ROWS)
    rows = H * ROWS
    return call(
        attend_kernel,
        [((ROWS, H * DL), BF16), ((ROWS, H * DK), BF16), ((PEERS, OWN, DK), BF16)]
        + [((2, *seg), BF16)] + [(seg, F32)] * 3,
        [SMEM] * 2 + [VMEM] * 11,
        place, count, index, w4, w2, swap, own, mine, mates, *stacked,
        scratch=[
            pltpu.VMEM((DK + 2 * PAD, KEYS), BF16),
            pltpu.VMEM((rows, KEYS), BF16),
            pltpu.VMEM((rows, KEYS), BF16),
            pltpu.VMEM((rows // 2, KEYS), F32),
        ],
        flops=2 * rows * KEYS * 6 * DK,
        mib=MIB,
    )


def stack(query_rows, grad_rows):
    rows = H * ROWS
    shapes = ((rows, DK + PAD), (rows, DL), (DK, rows), (DL, rows))
    return call(stack_kernel, [(shape, BF16) for shape in shapes], [VMEM] * 2, query_rows, grad_rows, mib=12)


def shifted(block, distance):
    devices = range(PEERS)
    route = [(i - distance, i) for i in devices if i - distance in devices]
    return lax.ppermute(block, SEQ, route)


def swapped(block):
    return lax.ppermute(block, "c", [(0, 1), (1, 0)])


def exchange(pieces, axis):
    return lax.all_to_all(pieces, axis, 0, 0, tiled=True)


def step(queries, latents, cotangent, comp_weight, sel_idx, sel_count):
    own = latents[0].T
    place = lax.axis_index(SEQ).astype(jnp.int32).reshape(1)
    seg = (DK, ROWS)
    pair = ((2, *seg), BF16)
    w2 = shifted(own, 2)
    w4 = shifted(own, 4)
    (pieces,) = call(compress_kernel, [((PEERS // 2, OWN, DK), BF16)], [VMEM] * 2, own, comp_weight, mib=56)
    mine = exchange(pieces, ("y", "x"))
    stacked = stack(queries[0], cotangent[0])
    mates = swapped(mine)
    (packed,) = call(pack_kernel, [pair], [SMEM] + [VMEM] * 3, place, own, w2, w4)
    attended, query_out, comp_pieces, swap_out, g4, g2, g0 = attend(
        place, sel_count, sel_idx[0], w4, w2, swapped(packed), own, mine, mates, stacked
    )
    comp_parts = exchange(comp_pieces, SEQ)
    swap_in = swapped(swap_out)
    send2, send4 = call(merge_kernel, [(seg, BF16)] * 2, [SMEM] + [VMEM] * 3, place, swap_in, g2, g4)
    r2, r4 = shifted(send2, -2), shifted(send4, -4)
    comp, part = call(
        weight_kernel, [((OWN, DK), F32), ((8, OWN, DK), BF16)], [VMEM] * 2, comp_parts, own
    )
    for axis in (ROW, "y", "z"):
        (part,) = call(sum_kernel, [((8, OWN, DK), BF16)], [VMEM], exchange(part, axis))
    weight_grad = exchange(part, ROW).reshape(CS, DK).astype(F32)
    (latent_grad,) = call(
        latent_kernel, [(seg, F32)], [SMEM] + [VMEM] * 6, place, comp, comp_weight, swap_in, g0, r2, r4
    )
    return (attended[None], query_out[None], latent_grad.T[None], weight_grad)


def solution(mesh):
    torus = Mesh(mesh.devices.reshape(mesh.shape["grp"], -1, 4, 2), ("z", "y", "x", "c"))
    split = P("z", SEQ, None)
    in_specs = (split, split, split, P(), split, P("z", SEQ))
    out_specs = (split, split, split, P())
    return jax.shard_map(step, mesh=torus, in_specs=in_specs, out_specs=out_specs, check_vma=False)
```

```python
import jax
import jax.numpy as jnp
from jax import lax
from jax.experimental import pallas as pl
from jax.experimental.pallas import tpu as pltpu
from jax.sharding import Mesh, PartitionSpec as P

DL = 512
DR = 64
H = 8
QB = 64
CS = 32
SEL = 64
WIN = 512
DK = 576

ROWS = 128
OWN = ROWS // CS
PEERS = 64
WKEYS = WIN + ROWS
KEYS = WKEYS + 2 * SEL
MIB = 28
PAD = DR

SEQ = ("y", "x", "c")
ROW = ("x", "c")

score_scale = 192.0 ** (-0.5)
F32 = jnp.float32
BF16 = jnp.bfloat16
VMEM = pl.BlockSpec(memory_space=pltpu.VMEM)
SMEM = pl.BlockSpec(memory_space=pltpu.SMEM)


def iota(shape, dim):
    return lax.broadcasted_iota(jnp.int32, shape, dim)


def dot_nn(a, b, **kw):
    return lax.dot_general(a, b, (((1,), (0,)), ((), ())), preferred_element_type=F32, **kw)


def dot_nt(a, b, **kw):
    return lax.dot_general(a, b, (((1,), (1,)), ((), ())), preferred_element_type=F32, **kw)


def dot_tn(a, b, **kw):
    return lax.dot_general(a, b, (((0,), (0,)), ((), ())), preferred_element_type=F32, **kw)


EXACT = dict(precision=lax.Precision.HIGHEST)


def spread_weight(weight):
    return dot_tn(weight, (iota((CS, ROWS), 1) % CS == iota((CS, ROWS), 0)).astype(F32), **EXACT)


def owner():
    return (iota((OWN, ROWS), 1) // CS == iota((OWN, ROWS), 0)).astype(F32)


def compress_kernel(own_ref, weight_ref, out_ref, rows_ref):
    rows = own_ref[...].astype(F32).T
    rows_ref[...] = rows.astype(BF16)
    weight = weight_ref[...]
    blocks = [rows[b * CS : (b + 1) * CS] * weight for b in range(OWN)]
    piece = jnp.concatenate([jnp.sum(block, axis=0, keepdims=True) for block in blocks], axis=0)
    out_ref[...] = jnp.broadcast_to(piece.astype(BF16)[None], out_ref.shape)


def pack_kernel(place_ref, own_ref, w2_ref, w4_ref, out_ref):
    first = place_ref[0] % 2 == 0
    w2 = w2_ref[...]
    out_ref[0] = jnp.where(first, w2, w4_ref[...])
    out_ref[1] = jnp.where(first, own_ref[...], w2)


def merge_kernel(place_ref, swap_ref, g2_ref, g4_ref, out2_ref, out4_ref):
    first = place_ref[0] % 2 == 0
    near, far = swap_ref[0].astype(F32), swap_ref[1].astype(F32)
    out2_ref[...] = (g2_ref[...] + jnp.where(first, far, near)).astype(BF16)
    out4_ref[...] = (g4_ref[...] + jnp.where(first, 0.0, far)).astype(BF16)


def stack_kernel(query_ref, grad_ref, query_out_ref, grad_out_ref, query_t_ref, grad_t_ref):
    for pair in range(H // 2):
        query_pair_t = query_ref[:, pair * 2 * DK : (pair + 1) * 2 * DK].T
        for odd in range(2):
            head = 2 * pair + odd
            rows = slice((odd * H // 2 + pair) * ROWS, (odd * H // 2 + pair + 1) * ROWS)
            start = pair * 2 * DK + odd * DL
            query_out_ref[rows, :] = query_ref[:, start : start + DK + PAD]
            query_t_ref[:, rows] = query_pair_t[odd * DK : (odd + 1) * DK]
            grad_rows = grad_ref[:, head * DL : (head + 1) * DL]
            grad_out_ref[rows, :] = grad_rows
            grad_t_ref[:, rows] = grad_rows.T


def attend_kernel(
    place_ref, count_ref, index_ref, w4_ref, w2_ref, swap_ref, own_ref, mine_ref, mates_ref, query_ref, grad_ref, query_t_ref, grad_t_ref,
    attended_ref, query_out_ref, comp_out_ref, swap_out_ref, g4_ref, g2_ref, g0_ref,
    key_ref, dscore_ref, prob_ref, bias_ref,
):
    place = place_ref[0]
    slot = iota((1, SEL), 1)
    chosen = [jnp.where(slot < count_ref[0, r], index_ref[r : r + 1, :], -1) for r in range(2)]
    chosen = jnp.concatenate(chosen, axis=1)
    key_ref[:PAD, :] = jnp.zeros((PAD, KEYS), BF16)
    key_ref[PAD + DK :, :] = jnp.zeros((PAD, KEYS), BF16)
    for i, ref in enumerate((w4_ref, swap_ref.at[0], w2_ref, swap_ref.at[1], own_ref)):
        key_ref[PAD : PAD + DK, i * ROWS : (i + 1) * ROWS] = ref[...]
    picks = (iota((OWN * PEERS, 2 * SEL), 0) == chosen).astype(F32).astype(BF16)
    row = iota((OWN * PEERS // 2, 2 * SEL), 0)
    picked_keys = jnp.zeros((DK, 2 * SEL), F32)
    for ref, core in ((mine_ref, place % 2), (mates_ref, 1 - place % 2)):
        picks_here = (2 * OWN * (row // OWN) + row % OWN + OWN * core == chosen).astype(F32).astype(BF16)
        picked_keys = picked_keys + dot_tn(ref[...].reshape(OWN * PEERS // 2, DK), picks_here)
    key_ref[PAD : PAD + DK, WKEYS:] = picked_keys.astype(BF16)

    heads = H // 2
    token = iota((heads * ROWS, KEYS), 0) % ROWS
    key = iota((heads * ROWS, KEYS), 1)
    near = (key <= token + WIN) & (key > token) & (key >= WIN - place * ROWS)
    picked = (key - WKEYS) // SEL == token // QB
    live = jnp.concatenate([jnp.zeros((1, WKEYS), jnp.int32), (chosen >= 0).astype(jnp.int32)], axis=1)
    live = jnp.broadcast_to(live, (heads * ROWS, KEYS)) > 0
    allowed = jnp.where(key < WKEYS, near.astype(jnp.int32), (picked & live).astype(jnp.int32)) > 0
    bias_ref[...] = jnp.where(allowed, 0.0, -1e30)
    values = key_ref[PAD : PAD + DL, :]

    grads = []
    for odd in range(2):
        rows = slice(odd * heads * ROWS, (odd + 1) * heads * ROWS)
        keys = key_ref[:DK + PAD, :] if odd else key_ref[PAD:, :]
        query_rows, grad_rows = query_ref[rows, :], grad_ref[rows, :]
        scores = dot_nn(query_rows, keys) * score_scale + bias_ref[...]
        expo = jnp.exp(scores - jnp.max(scores, axis=1, keepdims=True))
        weights = expo * (1.0 / jnp.sum(expo, axis=1, keepdims=True))
        rounded = weights.astype(BF16)
        prob_ref[rows, :] = rounded
        context = dot_nt(rounded, values)
        prob_grad = dot_nn(grad_rows, values)
        row_dot = jnp.sum(grad_rows.astype(F32) * context, axis=1, keepdims=True)
        dscore = (weights * (prob_grad - row_dot)).astype(BF16)
        dscore_ref[rows, :] = dscore
        grads.append(dot_nt(dscore, keys) * score_scale)
        for pair in range(heads):
            a = (2 * pair + odd) * DL
            attended_ref[:, a : a + DL] = context[pair * ROWS : (pair + 1) * ROWS].astype(BF16)
    for pair in range(heads):
        left = pair * 2 * DK
        even, odd = (g[pair * ROWS : (pair + 1) * ROWS] for g in grads)
        middle = even[:, DL:] + odd[:, : DK + PAD - DL]
        query_out_ref[:, left : left + DL] = even[:, :DL].astype(BF16)
        query_out_ref[:, left + DL : left + DK + PAD] = middle.astype(BF16)
        query_out_ref[:, left + DK + PAD : left + 2 * DK] = odd[:, DK + PAD - DL :].astype(BF16)

    dscore, rounded = dscore_ref[...], prob_ref[...]
    key_grad = dot_nn(query_t_ref[...], dscore) * score_scale
    value_grad = dot_nn(grad_t_ref[...], rounded)
    total = jnp.concatenate([key_grad[:DL] + value_grad, key_grad[DL:]], axis=0)
    for i, ref in enumerate((g4_ref, swap_out_ref.at[1], g2_ref, swap_out_ref.at[0], g0_ref)):
        ref[...] = total[:, i * ROWS : (i + 1) * ROWS].astype(ref.dtype)
    comp = dot_nt(picks, total[:, WKEYS:].astype(BF16))
    comp_out_ref[...] = comp.astype(BF16).reshape(comp_out_ref.shape)


def weight_kernel(comp_ref, rows_ref, comp_out_ref, weight_out_ref):
    comp = jnp.sum(comp_ref[...].astype(F32), axis=0)
    comp_out_ref[...] = comp
    part = jnp.zeros((CS, DK), F32)
    for b in range(OWN):
        part = part + comp[b : b + 1, :] * rows_ref[b * CS : (b + 1) * CS, :].astype(F32)
    part = part.astype(BF16)
    for i in range(weight_out_ref.shape[0]):
        weight_out_ref[i] = part[OWN * i : OWN * (i + 1)]


def latent_kernel(place_ref, comp_ref, weight_ref, swap_ref, g0_ref, r2_ref, r4_ref, out_ref):
    wide = dot_tn(comp_ref[...], owner(), **EXACT)
    near = jnp.where(place_ref[0] % 2 == 0, swap_ref[0].astype(F32), 0.0)
    total = g0_ref[...] + near + r2_ref[...].astype(F32) + r4_ref[...].astype(F32)
    out_ref[...] = total + wide * spread_weight(weight_ref[...])


def sum_kernel(part_ref, out_ref):
    total = jnp.sum(part_ref[...].astype(F32), axis=0, keepdims=True)
    out_ref[...] = jnp.broadcast_to(total, out_ref.shape).astype(out_ref.dtype)


def call(kernel, outs, in_specs, *args, scratch=(), flops=0, mib=8):
    shapes = [jax.ShapeDtypeStruct(shape, dtype) for shape, dtype in outs]
    nbytes = sum(a.size * a.dtype.itemsize for a in args) + sum(s.size * s.dtype.itemsize for s in shapes)
    return pl.pallas_call(
        kernel,
        out_shape=shapes,
        in_specs=in_specs,
        out_specs=[VMEM] * len(shapes),
        scratch_shapes=scratch,
        compiler_params=pltpu.CompilerParams(vmem_limit_bytes=mib << 20),
        cost_estimate=pl.CostEstimate(flops=flops, bytes_accessed=nbytes, transcendentals=0),
    )(*args)


def attend(place, count, index, w4, w2, swap, own, mine, mates, stacked):
    seg = (DK, ROWS)
    rows = H * ROWS
    return call(
        attend_kernel,
        [((ROWS, H * DL), BF16), ((ROWS, H * DK), BF16), ((PEERS, OWN, DK), BF16)]
        + [((2, *seg), BF16)] + [(seg, F32)] * 3,
        [SMEM] * 2 + [VMEM] * 11,
        place, count, index, w4, w2, swap, own, mine, mates, *stacked,
        scratch=[
            pltpu.VMEM((DK + 2 * PAD, KEYS), BF16),
            pltpu.VMEM((rows, KEYS), BF16),
            pltpu.VMEM((rows, KEYS), BF16),
            pltpu.VMEM((rows // 2, KEYS), F32),
        ],
        flops=2 * rows * KEYS * 6 * DK,
        mib=MIB,
    )


def stack(query_rows, grad_rows):
    rows = H * ROWS
    shapes = ((rows, DK + PAD), (rows, DL), (DK, rows), (DL, rows))
    return call(stack_kernel, [(shape, BF16) for shape in shapes], [VMEM] * 2, query_rows, grad_rows, mib=12)


def shifted(block, distance):
    devices = range(PEERS)
    route = [(i - distance, i) for i in devices if i - distance in devices]
    return lax.ppermute(block, SEQ, route)


def swapped(block):
    return lax.ppermute(block, "c", [(0, 1), (1, 0)])


def exchange(pieces, axis):
    return lax.all_to_all(pieces, axis, 0, 0, tiled=True)


def step(queries, latents, cotangent, comp_weight, sel_idx, sel_count):
    own = latents[0].T
    place = lax.axis_index(SEQ).astype(jnp.int32).reshape(1)
    seg = (DK, ROWS)
    pair = ((2, *seg), BF16)
    w2 = shifted(own, 2)
    w4 = shifted(own, 4)
    pieces, rows = call(
        compress_kernel,
        [((PEERS // 2, OWN, DK), BF16), ((ROWS, DK), BF16)],
        [VMEM] * 2,
        own, comp_weight,
        mib=56,
    )
    mine = exchange(pieces, ("y", "x"))
    stacked = stack(queries[0], cotangent[0])
    mates = swapped(mine)
    (packed,) = call(pack_kernel, [pair], [SMEM] + [VMEM] * 3, place, own, w2, w4)
    swap = swapped(packed)
    attended, query_out, comp_pieces, swap_out, g4, g2, g0 = attend(
        place, sel_count, sel_idx[0], w4, w2, swap, own, mine, mates, stacked
    )
    comp_parts = exchange(comp_pieces, SEQ)
    swap_in = swapped(swap_out)
    send2, send4 = call(merge_kernel, [(seg, BF16)] * 2, [SMEM] + [VMEM] * 3, place, swap_in, g2, g4)
    r2, r4 = shifted(send2, -2), shifted(send4, -4)
    comp, part = call(
        weight_kernel, [((OWN, DK), F32), ((8, OWN, DK), BF16)], [VMEM] * 2, comp_parts, rows
    )
    for axis in (ROW, "y", "z"):
        (part,) = call(sum_kernel, [((8, OWN, DK), BF16)], [VMEM], exchange(part, axis))
    weight_grad = exchange(part, ROW).reshape(CS, DK).astype(F32)
    (latent_grad,) = call(
        latent_kernel, [(seg, F32)], [SMEM] + [VMEM] * 6, place, comp, comp_weight, swap_in, g0, r2, r4
    )
    return (attended[None], query_out[None], latent_grad.T[None], weight_grad)


def solution(mesh):
    torus = Mesh(mesh.devices.reshape(mesh.shape["grp"], -1, 4, 2), ("z", "y", "x", "c"))
    split = P("z", SEQ, None)
    in_specs = (split, split, split, P(), split, P("z", SEQ))
    out_specs = (split, split, split, P())
    return jax.shard_map(step, mesh=torus, in_specs=in_specs, out_specs=out_specs, check_vma=False)
```
